256 devices in a mesh: seq: 32 (over z, x_hi, core), head: 8 (over y, x_lo).
Axes of the slice: x: 4 (x_hi: 2, x_lo: 2; x = x_hi * 2 + x_lo), y: 4, z: 8, core: 2. Of those that a mesh axis runs over, the one named last changes fastest.
Arguments:
- queries: bfloat16 [6144, 4096], P('seq', 'head'), may hold values from -64 to 64
- key_one: bfloat16 [6144, 128], P('seq'), may hold values from -6 to 6
- key_two: bfloat16 [6144, 128], P('seq'), may hold values from -6 to 6
- value_one: bfloat16 [6144, 128], P('seq'), may hold values from -6 to 6
- value_two: bfloat16 [6144, 128], P('seq'), may hold values from -6 to 6
- residual_in: bfloat16 [6144, 4096], P(('seq', 'head')), may hold values from -6 to 6
- out_weight: bfloat16 [4096, 4096], P('head'), may hold values from -0.5 to 0.5
- norm_gain: float32 [4096], replicated, may hold values from 0.1 to 1.9
- gate_weight: bfloat16 [4096, 7168], P('seq', 'head'), may hold values from -0.09375 to 0.09375
- up_weight: bfloat16 [4096, 7168], P('seq', 'head'), may hold values from -0.09375 to 0.09375
Outputs:
- residual_out: bfloat16 [6144, 4096], P(('seq', 'head'))
- hidden: bfloat16 [6144, 7168], P('seq', 'head')
The draws below stay inside these ranges and needn't reach their ends.
All inputs are finite; a program needn't handle non-finite values.
Results may differ from the reference program's by a relative error of at most 0.02.
Values may be sent and summed in bfloat16 or wider, within the bound.
No kernel may reach another device: no remote copies, remote signals or barrier semaphores. Data moves between devices by JAX's collectives and lax.ppermute only.
A program may use at most 64 MiB of HBM per device.

```python
import math
import jax
import jax.numpy as jnp
from jax import lax

D = 4096
HEADS = 32
HD = 128
W1 = 512
W2 = 32
FF = 7168
TOKENS = 6144


def shared_keys(key):
    first = jnp.clip(jax.random.normal(jax.random.fold_in(key, 11), (TOKENS, HD), jnp.float32), -6.0, 6.0)
    second = jnp.clip(jax.random.normal(jax.random.fold_in(key, 12), (TOKENS, HD), jnp.float32), -6.0, 6.0)
    return (first, second)


def draw_key_one(key, part):
    return shared_keys(key)[0].astype(jnp.bfloat16)


def draw_key_two(key, part):
    return shared_keys(key)[1].astype(jnp.bfloat16)


def draw_queries(key, part):
    drawn = jnp.clip(jax.random.normal(jax.random.fold_in(key, 14), (TOKENS, HEADS * HD), jnp.float32), -6.0, 6.0)
    return drawn.astype(jnp.bfloat16)


def block_scale(own_key, extent, pieces, least, top_value):
    level = 1.0
    for dim, parts in pieces:
        heights = jax.random.uniform(jax.random.fold_in(jax.random.fold_in(own_key, 6), dim), (parts,), jnp.float32, least / len(pieces), top_value / len(pieces))
        level = level * jnp.repeat(jnp.exp(heights), extent[dim] // parts).reshape((-1,) + (1,) * (len(extent) - 1 - dim))
    return level


def scatter_about(key, dims, scale, most, cuts=(), kind=jnp.bfloat16):
    gain = block_scale(key, dims, cuts, -0.22, 0.18) if cuts else 1.0
    drawn = jax.random.normal(key, dims, jnp.float32) * scale * gain
    return jnp.minimum(jnp.maximum(drawn, -most), most).astype(kind)


def setup_inputs(seed: int = 0) -> dict:
    key_of = jax.random.split(jax.random.key(seed), 11)
    return {
        "queries": draw_queries(jax.random.fold_in(key_of[10], 71), 0),
        "key_one": draw_key_one(jax.random.fold_in(key_of[10], 71), 0),
        "key_two": draw_key_two(jax.random.fold_in(key_of[10], 71), 0),
        "value_one": scatter_about(key_of[3], (TOKENS, HD), 1.0, 6.0, ((0, 32),)),
        "value_two": scatter_about(key_of[4], (TOKENS, HD), 1.0, 6.0, ((0, 32),)),
        "residual_in": scatter_about(key_of[5], (TOKENS, D), 1.0, 6.0, ((0, 256),)),
        "out_weight": scatter_about(key_of[6], (HEADS * HD, D), (HEADS * HD // 32) ** -0.5, 0.5, ((0, 8),)),
        "norm_gain": jnp.clip(1.0 + 0.18 * jax.random.normal(key_of[7], (D,), jnp.float32), 0.1, 1.9),
        "gate_weight": scatter_about(key_of[8], (D, FF), D ** -0.5, 0.09375, ((0, 32), (1, 8))),
        "up_weight": scatter_about(key_of[9], (D, FF), D ** -0.5, 0.09375, ((0, 32), (1, 8))),
    }


def normalize(summed, norm_gain):
    mean_square = lax.optimization_barrier(jnp.mean(summed * summed, axis=1, keepdims=True))
    scaled = summed * lax.rsqrt(mean_square + 1e-05) * norm_gain.astype(jnp.float32)
    return scaled.astype(jnp.bfloat16)

def windows(part, row_count):
    span = part.shape[0] - row_count + 1
    return jnp.stack([part[span - 1 - offset:span - 1 - offset + row_count] for offset in range(span)], axis=1)

def attention(queries, key_one, key_two, value_one, value_two):
    width = HD
    span = W2
    reach = W1 - 1
    block_rows = math.gcd(TOKENS, 32)
    factor = 2.5 * width ** (-0.5)
    far_keys = jnp.concatenate([jnp.zeros((reach, width), key_one.dtype), key_one], axis=0)
    far_values = jnp.concatenate([jnp.zeros((reach, width), value_one.dtype), value_one], axis=0)
    near_keys = jnp.concatenate([jnp.zeros((span - 1, width), key_two.dtype), key_two], axis=0)
    near_values = jnp.concatenate([jnp.zeros((span - 1, width), value_two.dtype), value_two], axis=0)
    grouped = queries.reshape(TOKENS, HEADS, width)

    def one_block(begin):
        query_block = lax.dynamic_slice_in_dim(grouped, begin, block_rows, 0)
        near_key_block = windows(lax.dynamic_slice_in_dim(near_keys, begin, block_rows + span - 1, 0), block_rows)
        near_value_block = windows(lax.dynamic_slice_in_dim(near_values, begin, block_rows + span - 1, 0), block_rows)
        key_block = lax.dynamic_slice_in_dim(far_keys, begin, block_rows + reach, 0)
        value_block = lax.dynamic_slice_in_dim(far_values, begin, block_rows + reach, 0)
        paired = (query_block.astype(jnp.float32)[:, :, None, :] * near_key_block.astype(jnp.float32)[:, None, :, :]).astype(jnp.bfloat16)
        logits = jnp.einsum('bhsd,cd->bhsc', paired.astype(jnp.float32), key_block.astype(jnp.float32)) * factor
        local = jnp.arange(block_rows, dtype=jnp.int32)[:, None]
        column = jnp.arange(block_rows + reach, dtype=jnp.int32)[None, :]
        query_pos = begin + local
        key_pos = begin - reach + column
        inside = (key_pos <= query_pos) & (key_pos >= query_pos - reach) & (key_pos >= 0)
        earlier_ok = query_pos - jnp.arange(span, dtype=jnp.int32)[None, :] >= 0
        valid = inside[:, None, None, :] & earlier_ok[:, None, :, None]
        masked = jnp.where(valid, logits, -jnp.inf)
        highest = lax.optimization_barrier(jnp.max(masked, axis=(2, 3), keepdims=True))
        expo = jnp.exp(masked - highest)
        probs = (expo / lax.optimization_barrier(jnp.sum(expo, axis=(2, 3), keepdims=True))).astype(jnp.bfloat16)
        mixed = jnp.einsum('bhsc,cd->bhsd', probs.astype(jnp.float32), value_block.astype(jnp.float32))
        combined = lax.optimization_barrier(jnp.sum(mixed * near_value_block.astype(jnp.float32)[:, None, :, :], axis=2))
        return combined.astype(jnp.bfloat16)
    begins = jnp.arange(TOKENS // block_rows, dtype=jnp.int32) * block_rows
    outputs = lax.map(one_block, begins)
    return outputs.reshape(TOKENS, HEADS * width)

def reference(queries, key_one, key_two, value_one, value_two, residual_in, out_weight, norm_gain, gate_weight, up_weight):
    attended = attention(queries, key_one, key_two, value_one, value_two)
    projected = jnp.dot(attended, out_weight, preferred_element_type=jnp.float32)
    summed = residual_in.astype(jnp.float32) + projected
    residual_out = summed.astype(jnp.bfloat16)
    normed = normalize(summed, norm_gain)
    gate_sum = jnp.dot(normed, gate_weight, preferred_element_type=jnp.float32)
    up_sum = jnp.dot(normed, up_weight, preferred_element_type=jnp.float32)
    hidden = (jax.nn.silu(gate_sum) * up_sum).astype(jnp.bfloat16)
    return (residual_out, hidden)
```

```python
import functools
import math

import jax
import jax.numpy as jnp
import numpy as np
from jax import lax
from jax.experimental import pallas as pl
from jax.experimental.pallas import tpu as pltpu
from jax.sharding import Mesh
from jax.sharding import PartitionSpec as P

LIMIT = 2.0 ** 90

def attention_kernel(heads, rank_ref, q_ref, far3_ref, far2_ref, far1_ref, own_ref, o_ref,
                     kt_ref, vx_ref, k2_ref, v2_ref, m_ref, acc_ref):
    rows, width = q_ref.shape[0], kt_ref.shape[0]
    span = 32
    third = far3_ref.shape[0]
    reach = third + 2 * rows
    total = reach + rows
    padded = kt_ref.shape[1]
    tile = 256
    rank = rank_ref[0]
    scale = 2.5 * width ** (-0.5) * math.log2(math.e)

    missing = jnp.maximum(reach - rows * rank, 0)
    k2_missing = jnp.where(rank == 0, span, 0)
    parts = [(far3_ref, 0, third), (far2_ref, third, rows), (far1_ref, third + rows, rows), (own_ref, reach, rows)]
    zero_pad = jnp.zeros((padded - total, width), jnp.bfloat16)
    keys = jnp.concatenate([ref[:, :width] for ref, _, _ in parts] + [zero_pad], axis=0)
    values = jnp.concatenate([ref[:, width:2 * width] for ref, _, _ in parts] + [zero_pad], axis=0)
    first = jnp.where(rank == 0, own_ref[0:16, :width].astype(jnp.float32),
             jnp.where(rank == 1, far1_ref[0:16, :width].astype(jnp.float32), far2_ref[0:16, :width].astype(jnp.float32)))[0:1]
    pos = lax.broadcasted_iota(jnp.int32, (padded, width), 0)
    absent = pos < missing
    keys = jnp.where(absent, jnp.broadcast_to(first, keys.shape), keys.astype(jnp.float32))
    kt_ref[...] = keys.T.astype(jnp.bfloat16)
    vx_ref[:, :width] = jnp.where(absent, 0.0, values.astype(jnp.float32)).astype(jnp.bfloat16)
    vx_ref[:, width:] = jnp.where(absent, 0.0, 1.0).astype(jnp.bfloat16)

    own2k = own_ref[:, 2 * width:3 * width].astype(jnp.float32)
    own2v = own_ref[:, 3 * width:4 * width].astype(jnp.float32)
    near2k = far1_ref[rows - span:, 2 * width:3 * width].astype(jnp.float32)
    near2v = far1_ref[rows - span:, 3 * width:4 * width].astype(jnp.float32)
    start = rank == 0
    k2 = jnp.concatenate([jnp.where(start, jnp.broadcast_to(own2k[0:1], near2k.shape), near2k), own2k], axis=0)
    v2 = jnp.concatenate([jnp.where(start, 0.0, near2v), own2v], axis=0)
    there = jnp.concatenate([jnp.where(start, 0.0, jnp.ones_like(near2v)), jnp.ones_like(own2v)], axis=0)
    for shift in range(8):
        kept = span + rows - shift
        k2_ref[shift, shift:] = k2[:kept]
        v2_ref[shift, shift:, :width] = v2[:kept]
        v2_ref[shift, shift:, width:] = there[:kept]

    def window(ref, offset):
        return ref[offset % 8, pl.ds(pl.multiple_of(span - offset // 8 * 8, 8), rows), :]

    row = lax.broadcasted_iota(jnp.int32, (rows, tile), 0)
    col = lax.broadcasted_iota(jnp.int32, (rows, tile), 1)
    early = col > row
    dot = functools.partial(jnp.dot, preferred_element_type=jnp.float32)

    def logits(offset, h):
        k2 = window(k2_ref, offset).astype(jnp.bfloat16)
        pair = q_ref[:, h * width:(h + 1) * width] * k2
        s = [dot(pair, kt_ref[:, i * tile:(i + 1) * tile]) for i in range(3)]
        return jnp.where(early, s[0], s[2]), s[1]

    def highest(offset, h):
        ends, middle = logits(offset, h)
        return jnp.max(jnp.maximum(ends, middle), axis=1, keepdims=True)

    def run():
        acc_ref[...] = jnp.zeros_like(acc_ref)

        def step(offset, _):
            v2 = window(v2_ref, offset)
            for h in range(heads):
                m = m_ref[h]
                m2 = jnp.concatenate([m, m], axis=1)
                ends, middle = logits(offset, h)
                ends = jnp.exp2(ends * scale - m2)
                middle = jnp.exp2(middle * scale - m2).astype(jnp.bfloat16)
                p0 = jnp.where(early, ends, 0.0).astype(jnp.bfloat16)
                p2 = jnp.where(early, 0.0, ends).astype(jnp.bfloat16)
                r = dot(jnp.concatenate([p0, middle, p2], axis=1), vx_ref[...])
                acc_ref[h] += r * v2
            return 0

        lax.fori_loop(0, span, step, 0)

    for h in range(heads):
        m_ref[h] = jnp.broadcast_to(highest(0, h) * scale, (rows, width))
    run()
    worst = jnp.max(jnp.where(acc_ref[:, :, width:] < LIMIT, 0.0, 1.0))

    @pl.when(worst > 0.0)
    def _():
        def climb(offset, _):
            for h in range(heads):
                m_ref[h] = jnp.maximum(m_ref[h], jnp.broadcast_to(highest(offset, h) * scale, (rows, width)))
            return 0

        lax.fori_loop(1, span, climb, 0)
        run()

    for h in range(heads):
        a = acc_ref[h]
        o_ref[:, h * width:(h + 1) * width] = (a[:, :width] / a[:, width:]).astype(jnp.bfloat16)


def attend(queries, far3, far2, far1, own, rank, kernel=attention_kernel):
    rows, cols = queries.shape
    width = own.shape[1] // 4
    heads = cols // width
    vm = pl.BlockSpec(memory_space=pltpu.VMEM)
    return pl.pallas_call(
        functools.partial(kernel, heads),
        out_shape=jax.ShapeDtypeStruct((rows, cols), jnp.bfloat16),
        in_specs=[pl.BlockSpec(memory_space=pltpu.SMEM)] + [vm] * 5,
        out_specs=vm,
        scratch_shapes=[
            pltpu.VMEM((width, 768), jnp.bfloat16),
            pltpu.VMEM((768, 2 * width), jnp.bfloat16),
            pltpu.VMEM((8, rows + 32, width), jnp.float32),
            pltpu.VMEM((8, rows + 32, 2 * width), jnp.float32),
            pltpu.VMEM((heads, rows, width), jnp.float32),
            pltpu.VMEM((heads, rows, 2 * width), jnp.float32),
        ],
        compiler_params=pltpu.CompilerParams(vmem_limit_bytes=48 * 2**20),
        cost_estimate=pl.CostEstimate(flops=30_000_000_000, bytes_accessed=2_000_000, transcendentals=12_000_000),
        name="attention",
    )(rank, queries, far3, far2, far1, own)


SEQ = ("z", "xh", "core")
HEAD = ("y", "xl")


def swapped(block, axis):
    return lax.ppermute(block, axis, [(0, 1), (1, 0)])


def from_behind(block, distance):
    devices = range(lax.axis_size(SEQ))
    route = [(i - distance, i) for i in devices if i - distance in devices]
    return lax.ppermute(block, SEQ, route)


def gathered_weight(gate_weight, up_weight):
    both = jnp.stack([gate_weight, up_weight], axis=0)
    mine = lax.all_to_all(both, "core", 0, 0, tiled=True)
    mine = mine.reshape(2 * gate_weight.shape[0], gate_weight.shape[1])
    other = swapped(mine, "xh")
    low = lax.axis_index("xh") == 0
    pair = jnp.concatenate([jnp.where(low, mine, other), jnp.where(low, other, mine)], axis=0)
    return lax.all_gather(pair, "z", axis=0, tiled=True)


def summed_on_arrival(array):
    rows, cols = array.shape
    devices = lax.axis_size(HEAD)
    tiles = array.reshape(devices, rows // devices, cols)
    arrived = lax.all_to_all(tiles, HEAD, split_axis=0, concat_axis=0, tiled=True)
    return arrived.astype(jnp.float32).sum(axis=0)


def sent_to_all(array):
    rows, cols = array.shape
    devices = lax.axis_size(HEAD)
    tiles = lax.all_to_all(jnp.broadcast_to(array[None], (devices, rows, cols)), HEAD, 0, 0, tiled=True)
    return tiles.reshape(devices * rows, cols)


def normalize(summed, norm_gain):
    mean_square = jnp.mean(summed * summed, axis=1, keepdims=True)
    scaled = summed * lax.rsqrt(mean_square + 1e-05) * norm_gain
    return scaled.astype(jnp.bfloat16)


def body(queries, key_one, key_two, value_one, value_two, residual_in, out_weight, norm_gain, gate_weight, up_weight):
    weight = gathered_weight(gate_weight, up_weight)
    rank = lax.axis_index(SEQ).astype(jnp.int32).reshape(1)
    rows = queries.shape[0]
    far = jnp.concatenate([key_one, value_one], axis=1)
    own = jnp.concatenate([far, key_two, value_two], axis=1)
    far1 = from_behind(own, 1)
    far2 = from_behind(far, 2)
    far3 = from_behind(far[3 * rows - 512 :], 3)
    attended = attend(queries, far3, far2, far1, own, rank)
    partial = jnp.dot(attended, out_weight, preferred_element_type=jnp.float32).astype(jnp.bfloat16)
    summed = residual_in.astype(jnp.float32) + summed_on_arrival(partial)
    residual_out = summed.astype(jnp.bfloat16)
    normed = sent_to_all(normalize(summed, norm_gain))
    others = swapped(normed, "core")
    ours = jnp.dot(normed, weight, preferred_element_type=jnp.float32)
    theirs = jnp.dot(others, weight, preferred_element_type=jnp.float32).astype(jnp.bfloat16)
    back = swapped(theirs, "core").astype(jnp.float32)
    gates = lax.axis_index("core") == 0
    gate_sum = jnp.where(gates, ours, back)
    up_sum = jnp.where(gates, back, ours)
    hidden = (jax.nn.silu(gate_sum) * up_sum).astype(jnp.bfloat16)
    return (residual_out, hidden)


def solution(mesh):
    fine = Mesh(np.asarray(mesh.devices).reshape(8, 2, 2, 4, 2), SEQ + HEAD)
    return jax.shard_map(
        body,
        mesh=fine,
        in_specs=(
            P(SEQ, HEAD),
            P(SEQ, None),
            P(SEQ, None),
            P(SEQ, None),
            P(SEQ, None),
            P(SEQ + HEAD, None),
            P(HEAD, None),
            P(),
            P(SEQ, HEAD),
            P(SEQ, HEAD),
        ),
        out_specs=(P(SEQ + HEAD, None), P(SEQ, HEAD)),
        check_vma=False,
    )
```

```python
import functools
import math

import jax
import jax.numpy as jnp
import numpy as np
from jax import lax
from jax.experimental import pallas as pl
from jax.experimental.pallas import tpu as pltpu
from jax.sharding import Mesh
from jax.sharding import PartitionSpec as P

LIMIT = 2.0 ** 90


def attention_kernel(heads, begin, stack, rank_ref, q_ref, far3_ref, far2_ref, far1_ref, own_ref, o_ref,
                     kt_ref, vx_ref, k2_ref, v2_ref, m_ref, acc_ref):
    count, width = q_ref.shape[0], kt_ref.shape[0]
    rows = own_ref.shape[0]
    groups = 8
    size, apart = count // groups, rows // groups
    span = 32
    third = far3_ref.shape[0]
    reach = third + 2 * rows
    total = reach + rows
    padded = kt_ref.shape[1]
    tile = 256
    rank = rank_ref[0]
    scale = 2.5 * width ** (-0.5) * math.log2(math.e)

    missing = jnp.maximum(reach - rows * rank, 0)
    k2_missing = jnp.where(rank == 0, span, 0)
    parts = [(far3_ref, 0, third), (far2_ref, third, rows), (far1_ref, third + rows, rows), (own_ref, reach, rows)]
    zero_pad = jnp.zeros((padded - total, width), jnp.bfloat16)
    keys = jnp.concatenate([ref[:, :width] for ref, _, _ in parts] + [zero_pad], axis=0)
    values = jnp.concatenate([ref[:, width:2 * width] for ref, _, _ in parts] + [zero_pad], axis=0)
    first = jnp.where(rank == 0, own_ref[0:16, :width].astype(jnp.float32),
             jnp.where(rank == 1, far1_ref[0:16, :width].astype(jnp.float32), far2_ref[0:16, :width].astype(jnp.float32)))[0:1]
    pos = lax.broadcasted_iota(jnp.int32, (padded, width), 0)
    absent = pos < missing
    keys = jnp.where(absent, jnp.broadcast_to(first, keys.shape), keys.astype(jnp.float32))
    kt_ref[...] = keys.T.astype(jnp.bfloat16)
    vx_ref[:, :width] = jnp.where(absent, 0.0, values.astype(jnp.float32)).astype(jnp.bfloat16)
    vx_ref[:, width:] = jnp.where(absent, 0.0, 1.0).astype(jnp.bfloat16)

    own2k = own_ref[:, 2 * width:3 * width].astype(jnp.float32)
    own2v = own_ref[:, 3 * width:4 * width].astype(jnp.float32)
    near2k = far1_ref[rows - span:, 2 * width:3 * width].astype(jnp.float32)
    near2v = far1_ref[rows - span:, 3 * width:4 * width].astype(jnp.float32)
    start = rank == 0
    k2 = jnp.concatenate([jnp.where(start, jnp.broadcast_to(own2k[0:1], near2k.shape), near2k), own2k], axis=0)
    v2 = jnp.concatenate([jnp.where(start, 0.0, near2v), own2v], axis=0)
    there = jnp.concatenate([jnp.where(start, 0.0, jnp.ones_like(near2v)), jnp.ones_like(own2v)], axis=0)
    for shift in range(8):
        kept = span + rows - shift
        k2_ref[shift, shift:] = k2[:kept]
        v2_ref[shift, shift:, :width] = v2[:kept]
        v2_ref[shift, shift:, width:] = there[:kept]

    def window(ref, offset):
        base = span + begin - offset // 8 * 8
        return jnp.concatenate([ref[offset % 8, pl.ds(pl.multiple_of(base + apart * g, 8), size), :] for g in range(groups)], axis=0)

    def at(shape):
        index = lax.broadcasted_iota(jnp.int32, shape, 0) % count
        return index // size * apart + index % size + begin

    def is_early(copies):
        shape = (copies * heads * count, tile)
        return lax.broadcasted_iota(jnp.int32, shape, 1) > at(shape)

    dot = functools.partial(jnp.dot, preferred_element_type=jnp.float32)

    def logits(offsets):
        pairs = []
        for offset in offsets:
            k2 = window(k2_ref, offset).astype(jnp.bfloat16)
            pairs += [q_ref[:, h * width:(h + 1) * width] * k2 for h in range(heads)]
        pair = jnp.concatenate(pairs, axis=0)
        return [dot(pair, kt_ref[:, i * tile:(i + 1) * tile]) for i in range(3)]

    def highest(offset):
        first, middle, last = logits([offset])
        return jnp.max(jnp.maximum(jnp.where(is_early(1), first, last), middle), axis=1, keepdims=True)

    def run():
        acc_ref[...] = jnp.zeros_like(acc_ref)

        def step(index, _):
            offsets = [index * stack + i for i in range(stack)]
            early = is_early(stack)
            first, middle, last = logits(offsets)
            m2 = jnp.concatenate([jnp.concatenate([m_ref[...]] * 2, axis=1)] * stack, axis=0)
            ends = jnp.exp2(jnp.where(early, first, last) * scale - m2)
            middle = jnp.exp2(middle * scale - m2).astype(jnp.bfloat16)
            p0 = jnp.where(early, ends, 0.0).astype(jnp.bfloat16)
            p2 = jnp.where(early, 0.0, ends).astype(jnp.bfloat16)
            r = dot(jnp.concatenate([p0, middle, p2], axis=1), vx_ref[...])
            for i, offset in enumerate(offsets):
                v2 = window(v2_ref, offset)
                for h in range(heads):
                    begins = (i * heads + h) * count
                    acc_ref[h * count:(h + 1) * count] += r[begins:begins + count] * v2
            return 0

        lax.fori_loop(0, span // stack, step, 0)

    m_ref[...] = jnp.broadcast_to(highest(0) * scale, m_ref.shape)
    run()
    worst = jnp.max(jnp.where(acc_ref[:, width:] < LIMIT, 0.0, 1.0))

    @pl.when(worst > 0.0)
    def _():
        def climb(offset, _):
            m_ref[...] = jnp.maximum(m_ref[...], jnp.broadcast_to(highest(offset) * scale, m_ref.shape))
            return 0

        lax.fori_loop(1, span, climb, 0)
        run()

    for h in range(heads):
        a = acc_ref[h * count:(h + 1) * count]
        o_ref[:, h * width:(h + 1) * width] = (a[:, :width] / a[:, width:]).astype(jnp.bfloat16)


def attend(queries, far3, far2, far1, own, rank, begin, stack):
    count, cols = queries.shape
    rows, width = own.shape[0], own.shape[1] // 4
    heads = cols // width
    vm = pl.BlockSpec(memory_space=pltpu.VMEM)
    return pl.pallas_call(
        functools.partial(attention_kernel, heads, begin, stack),
        out_shape=jax.ShapeDtypeStruct((count, cols), jnp.bfloat16),
        in_specs=[pl.BlockSpec(memory_space=pltpu.SMEM)] + [vm] * 5,
        out_specs=vm,
        scratch_shapes=[
            pltpu.VMEM((width, 768), jnp.bfloat16),
            pltpu.VMEM((768, 2 * width), jnp.bfloat16),
            pltpu.VMEM((8, rows + 32, width), jnp.float32),
            pltpu.VMEM((8, rows + 32, 2 * width), jnp.float32),
            pltpu.VMEM((heads * count, width), jnp.float32),
            pltpu.VMEM((heads * count, 2 * width), jnp.float32),
        ],
        compiler_params=pltpu.CompilerParams(vmem_limit_bytes=48 * 2**20),
        cost_estimate=pl.CostEstimate(
            flops=count * heads * 32 * 1536 * 512, bytes_accessed=2_000_000, transcendentals=count * heads * 32 * 512
        ),
        name="attention",
    )(rank, queries, far3, far2, far1, own)


SEQ = ("z", "xh", "core")
HEAD = ("y", "xl")
PARTS = ((16, 8, 2), (0, 16, 1))
EARLY = 256


def swapped(block, axis):
    return lax.ppermute(block, axis, [(0, 1), (1, 0)])


def in_turn(axis, mine, other, dim):
    first = lax.axis_index(axis) == 0
    return jnp.concatenate([jnp.where(first, mine, other), jnp.where(first, other, mine)], axis=dim)


def from_behind(block, distance):
    devices = range(lax.axis_size(SEQ))
    route = [(i - distance, i) for i in devices if i - distance in devices]
    return lax.ppermute(block, SEQ, route)


def over_heads(tiles):
    return lax.all_to_all(tiles, HEAD, 0, 0, tiled=True)


def normalize(summed, norm_gain):
    mean_square = jnp.mean(summed * summed, axis=1, keepdims=True)
    scaled = summed * lax.rsqrt(mean_square + 1e-05) * norm_gain
    return scaled.astype(jnp.bfloat16)


def body(queries, key_one, key_two, value_one, value_two, residual_in, out_weight, norm_gain, gate_weight, up_weight):
    rows, cols = queries.shape
    peers = lax.axis_size(HEAD)
    apart = rows // peers
    planes = lax.axis_size("z")
    gates = lax.axis_index("core") == 0
    kept = jnp.where(gates, gate_weight, up_weight)
    sent = jnp.where(gates, up_weight, gate_weight)
    far = jnp.concatenate([key_one, value_one], axis=1)
    own = jnp.concatenate([far, key_two, value_two], axis=1)
    mine = in_turn("core", kept, swapped(sent, "core"), 0)
    width = mine.shape[1]
    early, late = mine[:, width - EARLY :], mine[:, : width - EARLY]
    early = lax.all_gather(early, "z", axis=0, tiled=True)
    late_other = swapped(late, "xh")
    rank = lax.axis_index(SEQ).astype(jnp.int32).reshape(1)
    far1 = from_behind(own, 1)
    far2 = from_behind(far, 2)
    far3 = from_behind(far[3 * rows - 512 :], 3)
    grouped = queries.reshape(peers, apart, cols)
    residuals, normed, partials = {}, [], []
    for begin, size, stack in PARTS:
        part = grouped[:, begin : begin + size].reshape(peers * size, cols)
        if partials:
            part, _ = lax.optimization_barrier((part, partials[0]))
        attended = attend(part, far3, far2, far1, own, rank, begin, stack)
        if not partials:
            attended, early, late_other = lax.optimization_barrier((attended, early, late_other))
            late = lax.all_gather(in_turn("xh", late, late_other, 0), "z", axis=0, tiled=True)
            early_other = swapped(early, "xh")
        partials.append(jnp.dot(attended, out_weight, preferred_element_type=jnp.float32).astype(jnp.bfloat16))
    for (begin, size, _), partial in zip(PARTS, partials):
        arrived = over_heads(partial.reshape(peers, size, -1))
        arrived = arrived.astype(jnp.float32).sum(axis=0)
        summed = residual_in[begin : begin + size].astype(jnp.float32) + arrived
        residuals[begin] = summed.astype(jnp.bfloat16)
        own_rows = normalize(summed, norm_gain)
        tiles = jnp.broadcast_to(own_rows[None], (peers, *own_rows.shape))
        normed.append(over_heads(tiles).reshape(peers * size, -1))
    residual_out = jnp.concatenate([residuals[begin] for begin in sorted(residuals)], axis=0)
    early, early_other = (a.reshape(planes, 1, -1, EARLY) for a in (early, early_other))
    early = in_turn("xh", early, early_other, 1).reshape(-1, EARLY)
    ours = jnp.concatenate(normed, axis=0)
    theirs = jnp.concatenate([swapped(block, "core") for block in normed], axis=0)
    both = jnp.concatenate([ours, theirs], axis=0)
    product = jnp.concatenate(
        [jnp.dot(both, w, preferred_element_type=jnp.float32) for w in (late, early)], axis=1
    )
    back = swapped(product[rows:].astype(jnp.bfloat16), "core").astype(jnp.float32)
    gate_sum = jnp.where(gates, product[:rows], back)
    up_sum = jnp.where(gates, back, product[:rows])
    hidden = (jax.nn.silu(gate_sum) * up_sum).astype(jnp.bfloat16)
    pieces, at = {}, 0
    for begin, size, _ in PARTS:
        pieces[begin] = hidden[at : at + peers * size].reshape(peers, size, width)
        at += peers * size
    hidden = jnp.concatenate([pieces[begin] for begin in sorted(pieces)], axis=1).reshape(rows, width)
    return (residual_out, hidden)


def solution(mesh):
    fine = Mesh(np.asarray(mesh.devices).reshape(8, 2, 2, 4, 2), SEQ + HEAD)
    return jax.shard_map(
        body,
        mesh=fine,
        in_specs=(
            P(SEQ, HEAD),
            P(SEQ, None),
            P(SEQ, None),
            P(SEQ, None),
            P(SEQ, None),
            P(SEQ + HEAD, None),
            P(HEAD, None),
            P(),
            P(SEQ, HEAD),
            P(SEQ, HEAD),
        ),
        out_specs=(P(SEQ + HEAD, None), P(SEQ, HEAD)),
        check_vma=False,
    )
```

```python
import functools
import math

import jax
import jax.numpy as jnp
import numpy as np
from jax import lax
from jax.experimental import pallas as pl
from jax.experimental.pallas import tpu as pltpu
from jax.sharding import Mesh
from jax.sharding import PartitionSpec as P

LIMIT = 2.0 ** 90


def attention_kernel(heads, begin, stack, rank_ref, q_ref, far3_ref, far2_ref, far1_ref, own_ref, o_ref,
                     kt_ref, vx_ref, k2_ref, v2_ref, m_ref, acc_ref):
    count, width = q_ref.shape[0], kt_ref.shape[0]
    rows = own_ref.shape[0]
    groups = 8
    size, apart = count // groups, rows // groups
    span = 32
    third = far3_ref.shape[0]
    reach = third + 2 * rows
    total = reach + rows
    padded = kt_ref.shape[1]
    tile = 256
    rank = rank_ref[0]
    scale = 2.5 * width ** (-0.5) * math.log2(math.e)

    missing = jnp.maximum(reach - rows * rank, 0)
    k2_missing = jnp.where(rank == 0, span, 0)
    parts = [(far3_ref, 0, third), (far2_ref, third, rows), (far1_ref, third + rows, rows), (own_ref, reach, rows)]
    zero_pad = jnp.zeros((padded - total, width), jnp.bfloat16)
    keys = jnp.concatenate([ref[:, :width] for ref, _, _ in parts] + [zero_pad], axis=0)
    values = jnp.concatenate([ref[:, width:2 * width] for ref, _, _ in parts] + [zero_pad], axis=0)
    first = jnp.where(rank == 0, own_ref[0:16, :width].astype(jnp.float32),
             jnp.where(rank == 1, far1_ref[0:16, :width].astype(jnp.float32), far2_ref[0:16, :width].astype(jnp.float32)))[0:1]
    pos = lax.broadcasted_iota(jnp.int32, (padded, width), 0)
    absent = pos < missing
    keys = jnp.where(absent, jnp.broadcast_to(first, keys.shape), keys.astype(jnp.float32))
    kt_ref[...] = keys.T.astype(jnp.bfloat16)
    vx_ref[:, :width] = jnp.where(absent, 0.0, values.astype(jnp.float32)).astype(jnp.bfloat16)
    vx_ref[:, width:] = jnp.where(absent, 0.0, 1.0).astype(jnp.bfloat16)

    own2k = own_ref[:, 2 * width:3 * width].astype(jnp.float32)
    own2v = own_ref[:, 3 * width:4 * width].astype(jnp.float32)
    near2k = far1_ref[rows - span:, 2 * width:3 * width].astype(jnp.float32)
    near2v = far1_ref[rows - span:, 3 * width:4 * width].astype(jnp.float32)
    start = rank == 0
    k2 = jnp.concatenate([jnp.where(start, jnp.broadcast_to(own2k[0:1], near2k.shape), near2k), own2k], axis=0)
    v2 = jnp.concatenate([jnp.where(start, 0.0, near2v), own2v], axis=0)
    there = jnp.concatenate([jnp.where(start, 0.0, jnp.ones_like(near2v)), jnp.ones_like(own2v)], axis=0)
    for shift in range(8):
        kept = span + rows - shift
        k2_ref[shift, shift:] = k2[:kept]
        v2_ref[shift, shift:, :width] = v2[:kept]
        v2_ref[shift, shift:, width:] = there[:kept]

    def window(ref, offset):
        base = span + begin - offset // 8 * 8
        return jnp.concatenate([ref[offset % 8, pl.ds(pl.multiple_of(base + apart * g, 8), size), :] for g in range(groups)], axis=0)

    def at(shape):
        index = lax.broadcasted_iota(jnp.int32, shape, 0) % count
        return index // size * apart + index % size + begin

    def is_early(copies):
        shape = (copies * heads * count, tile)
        return lax.broadcasted_iota(jnp.int32, shape, 1) > at(shape)

    dot = functools.partial(jnp.dot, preferred_element_type=jnp.float32)

    def logits(offsets):
        pairs = []
        for offset in offsets:
            k2 = window(k2_ref, offset).astype(jnp.bfloat16)
            pairs += [q_ref[:, h * width:(h + 1) * width] * k2 for h in range(heads)]
        pair = jnp.concatenate(pairs, axis=0)
        return [dot(pair, kt_ref[:, i * tile:(i + 1) * tile]) for i in range(3)]

    def highest(offset):
        first, middle, last = logits([offset])
        return jnp.max(jnp.maximum(jnp.where(is_early(1), first, last), middle), axis=1, keepdims=True)

    def run():
        acc_ref[...] = jnp.zeros_like(acc_ref)

        def step(index, _):
            offsets = [index * stack + i for i in range(stack)]
            early = is_early(stack)
            first, middle, last = logits(offsets)
            m2 = jnp.concatenate([jnp.concatenate([m_ref[...]] * 2, axis=1)] * stack, axis=0)
            ends = jnp.exp2(jnp.where(early, first, last) * scale - m2)
            middle = jnp.exp2(middle * scale - m2).astype(jnp.bfloat16)
            p0 = jnp.where(early, ends, 0.0).astype(jnp.bfloat16)
            p2 = jnp.where(early, 0.0, ends).astype(jnp.bfloat16)
            r = dot(jnp.concatenate([p0, middle, p2], axis=1), vx_ref[...])
            for i, offset in enumerate(offsets):
                v2 = window(v2_ref, offset)
                for h in range(heads):
                    begins = (i * heads + h) * count
                    acc_ref[h * count:(h + 1) * count] += r[begins:begins + count] * v2
            return 0

        lax.fori_loop(0, span // stack, step, 0)

    m_ref[...] = jnp.broadcast_to(highest(0) * scale, m_ref.shape)
    run()
    worst = jnp.max(jnp.where(acc_ref[:, width:] < LIMIT, 0.0, 1.0))

    @pl.when(worst > 0.0)
    def _():
        def climb(offset, _):
            m_ref[...] = jnp.maximum(m_ref[...], jnp.broadcast_to(highest(offset) * scale, m_ref.shape))
            return 0

        lax.fori_loop(1, span, climb, 0)
        run()

    for h in range(heads):
        a = acc_ref[h * count:(h + 1) * count]
        o_ref[:, h * width:(h + 1) * width] = (a[:, :width] / a[:, width:]).astype(jnp.bfloat16)


def attend(queries, far3, far2, far1, own, rank, begin, stack):
    count, cols = queries.shape
    rows, width = own.shape[0], own.shape[1] // 4
    heads = cols // width
    vm = pl.BlockSpec(memory_space=pltpu.VMEM)
    return pl.pallas_call(
        functools.partial(attention_kernel, heads, begin, stack),
        out_shape=jax.ShapeDtypeStruct((count, cols), jnp.bfloat16),
        in_specs=[pl.BlockSpec(memory_space=pltpu.SMEM)] + [vm] * 5,
        out_specs=vm,
        scratch_shapes=[
            pltpu.VMEM((width, 768), jnp.bfloat16),
            pltpu.VMEM((768, 2 * width), jnp.bfloat16),
            pltpu.VMEM((8, rows + 32, width), jnp.float32),
            pltpu.VMEM((8, rows + 32, 2 * width), jnp.float32),
            pltpu.VMEM((heads * count, width), jnp.float32),
            pltpu.VMEM((heads * count, 2 * width), jnp.float32),
        ],
        compiler_params=pltpu.CompilerParams(vmem_limit_bytes=48 * 2**20),
        cost_estimate=pl.CostEstimate(
            flops=count * heads * 32 * 1536 * 512, bytes_accessed=2_000_000, transcendentals=count * heads * 32 * 512
        ),
        name="attention",
    )(rank, queries, far3, far2, far1, own)


SEQ = ("z", "xh", "core")
HEAD = ("y", "xl")


def prepare_kernel(core_ref, k1_ref, v1_ref, k2_ref, v2_ref, gate_ref, up_ref, own_ref, far_ref, last_ref, kept_ref, sent_ref):
    width = k1_ref.shape[1]
    skipped = k1_ref.shape[0] - last_ref.shape[0]
    for at, ref in enumerate((k1_ref, v1_ref, k2_ref, v2_ref)):
        own_ref[:, at * width : (at + 1) * width] = ref[...]
        if at < 2:
            far_ref[:, at * width : (at + 1) * width] = ref[...]
            last_ref[:, at * width : (at + 1) * width] = ref[skipped:, :]

    @pl.when(core_ref[0] == 0)
    def _():
        kept_ref[...] = gate_ref[...]
        sent_ref[...] = up_ref[...]

    @pl.when(core_ref[0] != 0)
    def _():
        kept_ref[...] = up_ref[...]
        sent_ref[...] = gate_ref[...]


def prepare(core, key_one, value_one, key_two, value_two, gate_weight, up_weight, last):
    rows, width = key_one.shape
    shape = lambda *dims: jax.ShapeDtypeStruct(dims, jnp.bfloat16)
    return pl.pallas_call(
        prepare_kernel,
        out_shape=(
            shape(rows, 4 * width),
            shape(rows, 2 * width),
            shape(last, 2 * width),
            shape(*gate_weight.shape),
            shape(*gate_weight.shape),
        ),
        in_specs=[pl.BlockSpec(memory_space=pltpu.SMEM)] + [pl.BlockSpec()] * 6,
        out_specs=(pl.BlockSpec(memory_space=pltpu.VMEM),) * 5,
        compiler_params=pltpu.CompilerParams(vmem_limit_bytes=60 * 2**20),
        name="prepare",
    )(core, key_one, value_one, key_two, value_two, gate_weight, up_weight)


def product_kernel(x_ref, w_ref, o_ref, total_ref):
    step = pl.program_id(0)
    part = jnp.dot(x_ref[...], w_ref[...], preferred_element_type=jnp.float32)

    @pl.when(step == 0)
    def _():
        total_ref[...] = part

    @pl.when(step > 0)
    def _():
        total_ref[...] += part

    @pl.when(step == pl.num_programs(0) - 1)
    def _():
        o_ref[...] = total_ref[...].astype(o_ref.dtype)


def product(x, w, dtype):
    rows, depth = x.shape
    width, block = w.shape[1], 512
    return pl.pallas_call(
        product_kernel,
        out_shape=jax.ShapeDtypeStruct((rows, width), dtype),
        grid=(depth // block,),
        in_specs=[pl.BlockSpec((rows, block), lambda i: (0, i)), pl.BlockSpec((block, width), lambda i: (i, 0))],
        out_specs=pl.BlockSpec((rows, width), lambda i: (0, 0)),
        scratch_shapes=[pltpu.VMEM((rows, width), jnp.float32)],
        compiler_params=pltpu.CompilerParams(vmem_limit_bytes=60 * 2**20),
        cost_estimate=pl.CostEstimate(
            flops=2 * rows * depth * width, bytes_accessed=2 * depth * (rows + width), transcendentals=0
        ),
    )(x, w)


def swapped(block, axis):
    return lax.ppermute(block, axis, [(0, 1), (1, 0)])


def in_turn(axis, mine, other, dim):
    first = lax.axis_index(axis) == 0
    return jnp.concatenate([jnp.where(first, mine, other), jnp.where(first, other, mine)], axis=dim)


def from_behind(block, distance):
    devices = range(lax.axis_size(SEQ))
    route = [(i - distance, i) for i in devices if i - distance in devices]
    return lax.ppermute(block, SEQ, route)


def over_heads(tiles):
    return lax.all_to_all(tiles, HEAD, 0, 0, tiled=True)


def normalize(summed, norm_gain):
    mean_square = jnp.mean(summed * summed, axis=1, keepdims=True)
    scaled = summed * lax.rsqrt(mean_square + 1e-05) * norm_gain
    return scaled.astype(jnp.bfloat16)


def body(queries, key_one, key_two, value_one, value_two, residual_in, out_weight, norm_gain, gate_weight, up_weight):
    rows, _ = queries.shape
    peers = lax.axis_size(HEAD)
    core = lax.axis_index("core").astype(jnp.int32)
    own, far, last, kept, sent = prepare(
        core.reshape(1), key_one, value_one, key_two, value_two, gate_weight, up_weight, 512 - 2 * rows
    )
    mine = in_turn("core", kept, swapped(sent, "core"), 0)
    other = swapped(mine, "xh")
    rank = lax.axis_index(SEQ).astype(jnp.int32).reshape(1)
    far1 = from_behind(own, 1)
    far2 = from_behind(far, 2)
    far3 = from_behind(last, 3)
    joined = in_turn("xh", mine, other, 0)
    weight = lax.all_gather(joined, "z", axis=0, tiled=True)
    attended = attend(queries, far3, far2, far1, own, rank, 0, 1)
    partial = jnp.dot(attended, out_weight, preferred_element_type=jnp.float32).astype(jnp.bfloat16)
    arrived = over_heads(partial.reshape(peers, rows // peers, -1)).astype(jnp.float32).sum(axis=0)
    summed = residual_in.astype(jnp.float32) + arrived
    residual_out = summed.astype(jnp.bfloat16)
    own_rows = normalize(summed, norm_gain)
    ours = over_heads(jnp.broadcast_to(own_rows[None], (peers, *own_rows.shape))).reshape(rows, -1)
    theirs = swapped(ours, "core")
    for_us = product(ours, weight, jnp.float32)
    for_them = product(theirs, weight, jnp.bfloat16)
    back = swapped(for_them, "core").astype(jnp.float32)
    gates = core == 0
    gate_sum = jnp.where(gates, for_us, back)
    up_sum = jnp.where(gates, back, for_us)
    hidden = (jax.nn.silu(gate_sum) * up_sum).astype(jnp.bfloat16)
    return (residual_out, hidden)


def solution(mesh):
    fine = Mesh(np.asarray(mesh.devices).reshape(8, 2, 2, 4, 2), SEQ + HEAD)
    return jax.shard_map(
        body,
        mesh=fine,
        in_specs=(
            P(SEQ, HEAD),
            P(SEQ, None),
            P(SEQ, None),
            P(SEQ, None),
            P(SEQ, None),
            P(SEQ + HEAD, None),
            P(HEAD, None),
            P(),
            P(SEQ, HEAD),
            P(SEQ, HEAD),
        ),
        out_specs=(P(SEQ + HEAD, None), P(SEQ, HEAD)),
        check_vma=False,
    )
```

```python
import functools
import math

import jax
import jax.numpy as jnp
import numpy as np
from jax import lax
from jax.experimental import pallas as pl
from jax.experimental.pallas import tpu as pltpu
from jax.sharding import Mesh
from jax.sharding import PartitionSpec as P

LIMIT = 2.0 ** 90


def attention_kernel(heads, begin, stack, rank_ref, q_ref, far3_ref, far2_ref, far1_ref, own_ref, wo_ref, o_ref,
                     kt_ref, vx_ref, k2_ref, v2_ref, m_ref, acc_ref, weight_ref, sem):
    fetch = pltpu.make_async_copy(wo_ref, weight_ref, sem)
    fetch.start()
    count, width = q_ref.shape[0], kt_ref.shape[0]
    rows = own_ref.shape[0]
    groups = 8
    size, apart = count // groups, rows // groups
    span = 32
    third = far3_ref.shape[0]
    reach = third + 2 * rows
    total = reach + rows
    padded = kt_ref.shape[1]
    tile = 256
    rank = rank_ref[0]
    scale = 2.5 * width ** (-0.5) * math.log2(math.e)

    missing = jnp.maximum(reach - rows * rank, 0)
    k2_missing = jnp.where(rank == 0, span, 0)
    parts = [(far3_ref, 0, third), (far2_ref, third, rows), (far1_ref, third + rows, rows), (own_ref, reach, rows)]
    zero_pad = jnp.zeros((padded - total, width), jnp.bfloat16)
    keys = jnp.concatenate([ref[:, :width] for ref, _, _ in parts] + [zero_pad], axis=0)
    values = jnp.concatenate([ref[:, width:2 * width] for ref, _, _ in parts] + [zero_pad], axis=0)
    first = jnp.where(rank == 0, own_ref[0:16, :width].astype(jnp.float32),
             jnp.where(rank == 1, far1_ref[0:16, :width].astype(jnp.float32), far2_ref[0:16, :width].astype(jnp.float32)))[0:1]
    pos = lax.broadcasted_iota(jnp.int32, (padded, width), 0)
    absent = pos < missing
    keys = jnp.where(absent, jnp.broadcast_to(first, keys.shape), keys.astype(jnp.float32))
    kt_ref[...] = keys.T.astype(jnp.bfloat16)
    vx_ref[:, :width] = jnp.where(absent, 0.0, values.astype(jnp.float32)).astype(jnp.bfloat16)
    vx_ref[:, width:] = jnp.where(absent, 0.0, 1.0).astype(jnp.bfloat16)

    own2k = own_ref[:, 2 * width:3 * width].astype(jnp.float32)
    own2v = own_ref[:, 3 * width:4 * width].astype(jnp.float32)
    near2k = far1_ref[rows - span:, 2 * width:3 * width].astype(jnp.float32)
    near2v = far1_ref[rows - span:, 3 * width:4 * width].astype(jnp.float32)
    start = rank == 0
    k2 = jnp.concatenate([jnp.where(start, jnp.broadcast_to(own2k[0:1], near2k.shape), near2k), own2k], axis=0)
    v2 = jnp.concatenate([jnp.where(start, 0.0, near2v), own2v], axis=0)
    there = jnp.concatenate([jnp.where(start, 0.0, jnp.ones_like(near2v)), jnp.ones_like(own2v)], axis=0)
    for shift in range(8):
        kept = span + rows - shift
        k2_ref[shift, shift:] = k2[:kept]
        v2_ref[shift, shift:, :width] = v2[:kept]
        v2_ref[shift, shift:, width:] = there[:kept]

    def window(ref, offset):
        base = span + begin - offset // 8 * 8
        return jnp.concatenate([ref[offset % 8, pl.ds(pl.multiple_of(base + apart * g, 8), size), :] for g in range(groups)], axis=0)

    def at(shape):
        index = lax.broadcasted_iota(jnp.int32, shape, 0) % count
        return index // size * apart + index % size + begin

    def is_early(copies):
        shape = (copies * heads * count, tile)
        return lax.broadcasted_iota(jnp.int32, shape, 1) > at(shape)

    dot = functools.partial(jnp.dot, preferred_element_type=jnp.float32)

    def logits(offsets):
        pairs = []
        for offset in offsets:
            k2 = window(k2_ref, offset).astype(jnp.bfloat16)
            pairs += [q_ref[:, h * width:(h + 1) * width] * k2 for h in range(heads)]
        pair = jnp.concatenate(pairs, axis=0)
        return [dot(pair, kt_ref[:, i * tile:(i + 1) * tile]) for i in range(3)]

    def highest(offset):
        first, middle, last = logits([offset])
        return jnp.max(jnp.maximum(jnp.where(is_early(1), first, last), middle), axis=1, keepdims=True)

    def run():
        acc_ref[...] = jnp.zeros_like(acc_ref)

        def step(index, _):
            offsets = [index * stack + i for i in range(stack)]
            early = is_early(stack)
            first, middle, last = logits(offsets)
            m2 = jnp.concatenate([jnp.concatenate([m_ref[...]] * 2, axis=1)] * stack, axis=0)
            ends = jnp.exp2(jnp.where(early, first, last) * scale - m2)
            middle = jnp.exp2(middle * scale - m2).astype(jnp.bfloat16)
            p0 = jnp.where(early, ends, 0.0).astype(jnp.bfloat16)
            p2 = jnp.where(early, 0.0, ends).astype(jnp.bfloat16)
            r = dot(jnp.concatenate([p0, middle, p2], axis=1), vx_ref[...])
            for i, offset in enumerate(offsets):
                v2 = window(v2_ref, offset)
                for h in range(heads):
                    begins = (i * heads + h) * count
                    acc_ref[h * count:(h + 1) * count] += r[begins:begins + count] * v2
            return 0

        lax.fori_loop(0, span // stack, step, 0)

    m_ref[...] = jnp.broadcast_to(highest(0) * scale, m_ref.shape)
    run()
    worst = jnp.max(jnp.where(acc_ref[:, width:] < LIMIT, 0.0, 1.0))

    @pl.when(worst > 0.0)
    def _():
        def climb(offset, _):
            m_ref[...] = jnp.maximum(m_ref[...], jnp.broadcast_to(highest(offset) * scale, m_ref.shape))
            return 0

        lax.fori_loop(1, span, climb, 0)
        run()

    parts = []
    for h in range(heads):
        a = acc_ref[h * count:(h + 1) * count]
        parts.append((a[:, :width] / a[:, width:]).astype(jnp.bfloat16))
    attended = jnp.concatenate(parts, axis=1)
    fetch.wait()
    piece = 1024
    for at in range(0, o_ref.shape[1], piece):
        o_ref[:, at:at + piece] = dot(attended, weight_ref[:, at:at + piece]).astype(jnp.bfloat16)


def attend(queries, far3, far2, far1, own, rank, out_weight, begin, stack):
    count, cols = queries.shape
    rows, width = own.shape[0], own.shape[1] // 4
    heads = cols // width
    vm = pl.BlockSpec(memory_space=pltpu.VMEM)
    return pl.pallas_call(
        functools.partial(attention_kernel, heads, begin, stack),
        out_shape=jax.ShapeDtypeStruct((count, out_weight.shape[1]), jnp.bfloat16),
        in_specs=[pl.BlockSpec(memory_space=pltpu.SMEM)] + [vm] * 5 + [pl.BlockSpec(memory_space=pl.ANY)],
        out_specs=vm,
        scratch_shapes=[
            pltpu.VMEM((width, 768), jnp.bfloat16),
            pltpu.VMEM((768, 2 * width), jnp.bfloat16),
            pltpu.VMEM((8, rows + 32, width), jnp.float32),
            pltpu.VMEM((8, rows + 32, 2 * width), jnp.float32),
            pltpu.VMEM((heads * count, width), jnp.float32),
            pltpu.VMEM((heads * count, 2 * width), jnp.float32),
            pltpu.VMEM(out_weight.shape, jnp.bfloat16),
            pltpu.SemaphoreType.DMA,
        ],
        compiler_params=pltpu.CompilerParams(vmem_limit_bytes=48 * 2**20),
        cost_estimate=pl.CostEstimate(
            flops=count * heads * 32 * 1536 * 512, bytes_accessed=6_000_000, transcendentals=count * heads * 32 * 512
        ),
        name="attention",
    )(rank, queries, far3, far2, far1, own, out_weight)


SEQ = ("z", "xh", "core")
HEAD = ("y", "xl")


def prepare_kernel(core_ref, k1_ref, v1_ref, k2_ref, v2_ref, gate_ref, up_ref, own_ref, far_ref, last_ref, kept_ref, sent_ref):
    width = k1_ref.shape[1]
    skipped = k1_ref.shape[0] - last_ref.shape[0]
    for at, ref in enumerate((k1_ref, v1_ref, k2_ref, v2_ref)):
        own_ref[:, at * width : (at + 1) * width] = ref[...]
        if at < 2:
            far_ref[:, at * width : (at + 1) * width] = ref[...]
            last_ref[:, at * width : (at + 1) * width] = ref[skipped:, :]

    @pl.when(core_ref[0] == 0)
    def _():
        kept_ref[...] = gate_ref[...]
        sent_ref[...] = up_ref[...]

    @pl.when(core_ref[0] != 0)
    def _():
        kept_ref[...] = up_ref[...]
        sent_ref[...] = gate_ref[...]


def prepare(core, key_one, value_one, key_two, value_two, gate_weight, up_weight, last):
    rows, width = key_one.shape
    shape = lambda *dims: jax.ShapeDtypeStruct(dims, jnp.bfloat16)
    return pl.pallas_call(
        prepare_kernel,
        out_shape=(
            shape(rows, 4 * width),
            shape(rows, 2 * width),
            shape(last, 2 * width),
            shape(*gate_weight.shape),
            shape(*gate_weight.shape),
        ),
        in_specs=[pl.BlockSpec(memory_space=pltpu.SMEM)] + [pl.BlockSpec()] * 6,
        out_specs=(pl.BlockSpec(memory_space=pltpu.VMEM),) * 5,
        compiler_params=pltpu.CompilerParams(vmem_limit_bytes=60 * 2**20),
        name="prepare",
    )(core, key_one, value_one, key_two, value_two, gate_weight, up_weight)


def product_kernel(place_ref, ours_ref, theirs_ref, near_ref, far_ref, us_ref, them_ref, w_ref, total_ref, sems):
    chunks, block, _ = w_ref.shape
    rows, half = us_ref.shape[0], block // 2
    planes = chunks // 2
    cross, core = place_ref[0], place_ref[1]
    sources = [(near_ref, plane) for plane in range(planes)] + [(far_ref, plane) for plane in range(planes)]
    copies = [
        pltpu.make_async_copy(ref.at[pl.ds(plane * block, block), :], w_ref.at[i], sems.at[i])
        for i, (ref, plane) in enumerate(sources)
    ]
    for copy in copies:
        copy.start()
    together = 4
    for first in range(0, chunks, together):
        columns = []
        for i in range(first, first + together):
            copies[i].wait()
            plane = i % planes
            side = cross if i < planes else 1 - cross
            for part in (core, 1 - core):
                at = pl.multiple_of(((plane * 2 + side) * 2 + part) * half, half)
                columns.append(
                    jnp.concatenate([ours_ref[:, pl.ds(at, half)], theirs_ref[:, pl.ds(at, half)]], axis=0)
                )
        x = jnp.concatenate(columns, axis=1)
        w = w_ref[first : first + together].reshape(together * block, w_ref.shape[2])
        part = jnp.dot(x, w, preferred_element_type=jnp.float32)
        if first == 0:
            total_ref[...] = part
        else:
            total_ref[...] += part
    us_ref[...] = total_ref[:rows]
    them_ref[...] = total_ref[rows:].astype(jnp.bfloat16)


def product(place, ours, theirs, near, far):
    rows, depth = ours.shape
    width, block = near.shape[1], 256
    vm, hbm = pl.BlockSpec(memory_space=pltpu.VMEM), pl.BlockSpec(memory_space=pl.ANY)
    return pl.pallas_call(
        product_kernel,
        out_shape=(jax.ShapeDtypeStruct((rows, width), jnp.float32), jax.ShapeDtypeStruct((rows, width), jnp.bfloat16)),
        in_specs=[pl.BlockSpec(memory_space=pltpu.SMEM), vm, vm, hbm, hbm],
        out_specs=(vm, vm),
        scratch_shapes=[
            pltpu.VMEM((depth // block, block, width), jnp.bfloat16),
            pltpu.VMEM((2 * rows, width), jnp.float32),
            pltpu.SemaphoreType.DMA((depth // block,)),
        ],
        compiler_params=pltpu.CompilerParams(vmem_limit_bytes=48 * 2**20),
        cost_estimate=pl.CostEstimate(
            flops=4 * rows * depth * width, bytes_accessed=2 * depth * (2 * rows + width), transcendentals=0
        ),
        name="product",
    )(place, ours, theirs, near, far)


def finish_kernel(place_ref, us_ref, back_ref, o_ref):
    def store(gate, up):
        o_ref[...] = (gate / (1.0 + jnp.exp(-gate)) * up).astype(jnp.bfloat16)

    @pl.when(place_ref[1] == 0)
    def _():
        store(us_ref[...], back_ref[...].astype(jnp.float32))

    @pl.when(place_ref[1] != 0)
    def _():
        store(back_ref[...].astype(jnp.float32), us_ref[...])


def finish(place, for_us, back):
    vm = pl.BlockSpec(memory_space=pltpu.VMEM)
    return pl.pallas_call(
        finish_kernel,
        out_shape=jax.ShapeDtypeStruct(back.shape, jnp.bfloat16),
        in_specs=[pl.BlockSpec(memory_space=pltpu.SMEM), vm, vm],
        out_specs=vm,
        compiler_params=pltpu.CompilerParams(vmem_limit_bytes=48 * 2**20),
        name="finish",
    )(place, for_us, back)


def swapped(block, axis):
    return lax.ppermute(block, axis, [(0, 1), (1, 0)])


def from_behind(block, distance):
    devices = range(lax.axis_size(SEQ))
    route = [(i - distance, i) for i in devices if i - distance in devices]
    return lax.ppermute(block, SEQ, route)


def over_heads(tiles):
    return lax.all_to_all(tiles, HEAD, 0, 0, tiled=True)


def normalize(summed, norm_gain):
    mean_square = jnp.mean(summed * summed, axis=1, keepdims=True)
    scaled = summed * lax.rsqrt(mean_square + 1e-05) * norm_gain
    return scaled.astype(jnp.bfloat16)


def body(queries, key_one, key_two, value_one, value_two, residual_in, out_weight, norm_gain, gate_weight, up_weight):
    rows, _ = queries.shape
    peers = lax.axis_size(HEAD)
    core = lax.axis_index("core").astype(jnp.int32)
    own, far, last, kept, sent = prepare(
        core.reshape(1), key_one, value_one, key_two, value_two, gate_weight, up_weight, 512 - 2 * rows
    )
    mine = jnp.concatenate([kept, swapped(sent, "core")], axis=0)
    near = lax.all_gather(mine, "z", axis=0, tiled=True)
    other = swapped(mine, "xh")
    place = jnp.stack([lax.axis_index("xh").astype(jnp.int32), core])
    rank = lax.axis_index(SEQ).astype(jnp.int32).reshape(1)
    far1 = from_behind(own, 1)
    far2 = from_behind(far, 2)
    far3 = from_behind(last, 3)
    far_weight = lax.all_gather(other, "z", axis=0, tiled=True)
    partial = attend(queries, far3, far2, far1, own, rank, out_weight, 0, 1)
    arrived = over_heads(partial.reshape(peers, rows // peers, -1)).astype(jnp.float32).sum(axis=0)
    summed = residual_in.astype(jnp.float32) + arrived
    residual_out = summed.astype(jnp.bfloat16)
    own_rows = normalize(summed, norm_gain)
    ours = over_heads(jnp.broadcast_to(own_rows[None], (peers, *own_rows.shape))).reshape(rows, -1)
    theirs = swapped(ours, "core")
    for_us, for_them = product(place, ours, theirs, near, far_weight)
    hidden = finish(place, for_us, swapped(for_them, "core"))
    return (residual_out, hidden)


def solution(mesh):
    fine = Mesh(np.asarray(mesh.devices).reshape(8, 2, 2, 4, 2), SEQ + HEAD)
    return jax.shard_map(
        body,
        mesh=fine,
        in_specs=(
            P(SEQ, HEAD),
            P(SEQ, None),
            P(SEQ, None),
            P(SEQ, None),
            P(SEQ, None),
            P(SEQ + HEAD, None),
            P(HEAD, None),
            P(),
            P(SEQ, HEAD),
            P(SEQ, HEAD),
        ),
        out_specs=(P(SEQ + HEAD, None), P(SEQ, HEAD)),
        check_vma=False,
    )
```

```python
import functools
import math

import jax
import jax.numpy as jnp
import numpy as np
from jax import lax
from jax.experimental import pallas as pl
from jax.experimental.pallas import tpu as pltpu
from jax.sharding import Mesh
from jax.sharding import PartitionSpec as P

LIMIT = 2.0 ** 90


def attention_kernel(heads, begin, stack, rank_ref, q_ref, far3_ref, far2_ref, far1_ref, own_ref, wo_ref, o_ref,
                     kt_ref, vx_ref, k2_ref, v2_ref, m_ref, acc_ref, weight_ref, sem):
    fetch = pltpu.make_async_copy(wo_ref, weight_ref, sem)
    fetch.start()
    count, width = q_ref.shape[0], kt_ref.shape[0]
    rows = own_ref.shape[0]
    groups = 8
    size, apart = count // groups, rows // groups
    span = 32
    third = far3_ref.shape[0]
    reach = third + 2 * rows
    total = reach + rows
    padded = kt_ref.shape[1]
    tile = 256
    rank = rank_ref[0]
    scale = 2.5 * width ** (-0.5) * math.log2(math.e)

    missing = jnp.maximum(reach - rows * rank, 0)
    k2_missing = jnp.where(rank == 0, span, 0)
    parts = [(far3_ref, 0, third), (far2_ref, third, rows), (far1_ref, third + rows, rows), (own_ref, reach, rows)]
    zero_pad = jnp.zeros((padded - total, width), jnp.bfloat16)
    keys = jnp.concatenate([ref[:, :width] for ref, _, _ in parts] + [zero_pad], axis=0)
    values = jnp.concatenate([ref[:, width:2 * width] for ref, _, _ in parts] + [zero_pad], axis=0)
    first = jnp.where(rank == 0, own_ref[0:16, :width].astype(jnp.float32),
             jnp.where(rank == 1, far1_ref[0:16, :width].astype(jnp.float32), far2_ref[0:16, :width].astype(jnp.float32)))[0:1]
    pos = lax.broadcasted_iota(jnp.int32, (padded, width), 0)
    absent = pos < missing
    keys = jnp.where(absent, jnp.broadcast_to(first, keys.shape), keys.astype(jnp.float32))
    kt_ref[...] = keys.T.astype(jnp.bfloat16)
    vx_ref[:, :width] = jnp.where(absent, 0.0, values.astype(jnp.float32)).astype(jnp.bfloat16)
    vx_ref[:, width:] = jnp.where(absent, 0.0, 1.0).astype(jnp.bfloat16)

    own2k = own_ref[:, 2 * width:3 * width].astype(jnp.float32)
    own2v = own_ref[:, 3 * width:4 * width].astype(jnp.float32)
    near2k = far1_ref[rows - span:, 2 * width:3 * width].astype(jnp.float32)
    near2v = far1_ref[rows - span:, 3 * width:4 * width].astype(jnp.float32)
    start = rank == 0
    k2 = jnp.concatenate([jnp.where(start, jnp.broadcast_to(own2k[0:1], near2k.shape), near2k), own2k], axis=0)
    v2 = jnp.concatenate([jnp.where(start, 0.0, near2v), own2v], axis=0)
    there = jnp.concatenate([jnp.where(start, 0.0, jnp.ones_like(near2v)), jnp.ones_like(own2v)], axis=0)
    for shift in range(8):
        kept = span + rows - shift
        k2_ref[shift, shift:] = k2[:kept]
        v2_ref[shift, shift:, :width] = v2[:kept]
        v2_ref[shift, shift:, width:] = there[:kept]

    def window(ref, offset):
        base = span + begin - offset // 8 * 8
        return jnp.concatenate([ref[offset % 8, pl.ds(pl.multiple_of(base + apart * g, 8), size), :] for g in range(groups)], axis=0)

    def at(shape):
        index = lax.broadcasted_iota(jnp.int32, shape, 0) % count
        return index // size * apart + index % size + begin

    def is_early(copies):
        shape = (copies * heads * count, tile)
        return lax.broadcasted_iota(jnp.int32, shape, 1) > at(shape)

    dot = functools.partial(jnp.dot, preferred_element_type=jnp.float32)

    def logits(offsets):
        pairs = []
        for offset in offsets:
            k2 = window(k2_ref, offset).astype(jnp.bfloat16)
            pairs += [q_ref[:, h * width:(h + 1) * width] * k2 for h in range(heads)]
        pair = jnp.concatenate(pairs, axis=0)
        return [dot(pair, kt_ref[:, i * tile:(i + 1) * tile]) for i in range(3)]

    def highest(offset):
        first, middle, last = logits([offset])
        return jnp.max(jnp.maximum(jnp.where(is_early(1), first, last), middle), axis=1, keepdims=True)

    def run():
        acc_ref[...] = jnp.zeros_like(acc_ref)

        def step(index, _):
            offsets = [index * stack + i for i in range(stack)]
            early = is_early(stack)
            first, middle, last = logits(offsets)
            m2 = jnp.concatenate([jnp.concatenate([m_ref[...]] * 2, axis=1)] * stack, axis=0)
            ends = jnp.exp2(jnp.where(early, first, last) * scale - m2)
            middle = jnp.exp2(middle * scale - m2).astype(jnp.bfloat16)
            p0 = jnp.where(early, ends, 0.0).astype(jnp.bfloat16)
            p2 = jnp.where(early, 0.0, ends).astype(jnp.bfloat16)
            r = dot(jnp.concatenate([p0, middle, p2], axis=1), vx_ref[...])
            for i, offset in enumerate(offsets):
                v2 = window(v2_ref, offset)
                for h in range(heads):
                    begins = (i * heads + h) * count
                    acc_ref[h * count:(h + 1) * count] += r[begins:begins + count] * v2
            return 0

        lax.fori_loop(0, span // stack, step, 0)

    m_ref[...] = jnp.broadcast_to(highest(0) * scale, m_ref.shape)
    run()
    worst = jnp.max(jnp.where(acc_ref[:, width:] < LIMIT, 0.0, 1.0))

    @pl.when(worst > 0.0)
    def _():
        def climb(offset, _):
            m_ref[...] = jnp.maximum(m_ref[...], jnp.broadcast_to(highest(offset) * scale, m_ref.shape))
            return 0

        lax.fori_loop(1, span, climb, 0)
        run()

    parts = []
    for h in range(heads):
        a = acc_ref[h * count:(h + 1) * count]
        parts.append((a[:, :width] / a[:, width:]).astype(jnp.bfloat16))
    attended = jnp.concatenate(parts, axis=1)
    fetch.wait()
    piece = 1024
    for at in range(0, o_ref.shape[1], piece):
        o_ref[:, at:at + piece] = dot(attended, weight_ref[:, at:at + piece]).astype(jnp.bfloat16)


def attend(queries, far3, far2, far1, own, rank, out_weight, begin, stack):
    count, cols = queries.shape
    rows, width = own.shape[0], own.shape[1] // 4
    heads = cols // width
    vm = pl.BlockSpec(memory_space=pltpu.VMEM)
    return pl.pallas_call(
        functools.partial(attention_kernel, heads, begin, stack),
        out_shape=jax.ShapeDtypeStruct((count, out_weight.shape[1]), jnp.bfloat16),
        in_specs=[pl.BlockSpec(memory_space=pltpu.SMEM)] + [vm] * 5 + [pl.BlockSpec(memory_space=pl.ANY)],
        out_specs=vm,
        scratch_shapes=[
            pltpu.VMEM((width, 768), jnp.bfloat16),
            pltpu.VMEM((768, 2 * width), jnp.bfloat16),
            pltpu.VMEM((8, rows + 32, width), jnp.float32),
            pltpu.VMEM((8, rows + 32, 2 * width), jnp.float32),
            pltpu.VMEM((heads * count, width), jnp.float32),
            pltpu.VMEM((heads * count, 2 * width), jnp.float32),
            pltpu.VMEM(out_weight.shape, jnp.bfloat16),
            pltpu.SemaphoreType.DMA,
        ],
        compiler_params=pltpu.CompilerParams(vmem_limit_bytes=48 * 2**20),
        cost_estimate=pl.CostEstimate(
            flops=count * heads * 32 * 1536 * 512, bytes_accessed=6_000_000, transcendentals=count * heads * 32 * 512
        ),
        name="attention",
    )(rank, queries, far3, far2, far1, own, out_weight)


SEQ = ("z", "xh", "core")
HEAD = ("y", "xl")


def prepare_kernel(core_ref, k1_ref, v1_ref, k2_ref, v2_ref, gate_ref, up_ref, own_ref, far_ref, last_ref, kept_ref, sent_ref):
    width = k1_ref.shape[1]
    skipped = k1_ref.shape[0] - last_ref.shape[0]
    for at, ref in enumerate((k1_ref, v1_ref, k2_ref, v2_ref)):
        own_ref[:, at * width : (at + 1) * width] = ref[...]
        if at < 2:
            far_ref[:, at * width : (at + 1) * width] = ref[...]
            last_ref[:, at * width : (at + 1) * width] = ref[skipped:, :]

    @pl.when(core_ref[0] == 0)
    def _():
        kept_ref[...] = gate_ref[...]
        sent_ref[...] = up_ref[...]

    @pl.when(core_ref[0] != 0)
    def _():
        kept_ref[...] = up_ref[...]
        sent_ref[...] = gate_ref[...]


def prepare(core, key_one, value_one, key_two, value_two, gate_weight, up_weight, last):
    rows, width = key_one.shape
    shape = lambda *dims: jax.ShapeDtypeStruct(dims, jnp.bfloat16)
    return pl.pallas_call(
        prepare_kernel,
        out_shape=(
            shape(rows, 4 * width),
            shape(rows, 2 * width),
            shape(last, 2 * width),
            shape(*gate_weight.shape),
            shape(*gate_weight.shape),
        ),
        in_specs=[pl.BlockSpec(memory_space=pltpu.SMEM)] + [pl.BlockSpec()] * 6,
        out_specs=(pl.BlockSpec(memory_space=pltpu.VMEM),) * 5,
        compiler_params=pltpu.CompilerParams(vmem_limit_bytes=60 * 2**20),
        name="prepare",
    )(core, key_one, value_one, key_two, value_two, gate_weight, up_weight)


def product_kernel(place_ref, ours_ref, theirs_ref, near_ref, far_ref, us_ref, them_ref, w_ref, total_ref, sems):
    chunks, block, _ = w_ref.shape
    rows, half = us_ref.shape[0], block // 2
    planes = chunks // 2
    cross, core = place_ref[0], place_ref[1]
    sources = [(near_ref, plane) for plane in range(planes)] + [(far_ref, plane) for plane in range(planes)]
    copies = [
        pltpu.make_async_copy(ref.at[pl.ds(plane * block, block), :], w_ref.at[i], sems.at[i])
        for i, (ref, plane) in enumerate(sources)
    ]
    for copy in copies:
        copy.start()
    together = 4
    for first in range(0, chunks, together):
        columns = []
        for i in range(first, first + together):
            copies[i].wait()
            plane = i % planes
            side = cross if i < planes else 1 - cross
            for part in (core, 1 - core):
                at = pl.multiple_of(((plane * 2 + side) * 2 + part) * half, half)
                columns.append(
                    jnp.concatenate([ours_ref[:, pl.ds(at, half)], theirs_ref[:, pl.ds(at, half)]], axis=0)
                )
        x = jnp.concatenate(columns, axis=1)
        w = w_ref[first : first + together].reshape(together * block, w_ref.shape[2])
        part = jnp.dot(x, w, preferred_element_type=jnp.float32)
        if first == 0:
            total_ref[...] = part
        else:
            total_ref[...] += part
    us_ref[...] = total_ref[:rows]
    them_ref[...] = total_ref[rows:].astype(jnp.bfloat16)


def product(place, ours, theirs, near, far):
    rows, depth = ours.shape
    width, block = near.shape[1], 256
    vm, hbm = pl.BlockSpec(memory_space=pltpu.VMEM), pl.BlockSpec(memory_space=pl.ANY)
    return pl.pallas_call(
        product_kernel,
        out_shape=(jax.ShapeDtypeStruct((rows, width), jnp.float32), jax.ShapeDtypeStruct((rows, width), jnp.bfloat16)),
        in_specs=[pl.BlockSpec(memory_space=pltpu.SMEM), vm, vm, hbm, hbm],
        out_specs=(vm, vm),
        scratch_shapes=[
            pltpu.VMEM((depth // block, block, width), jnp.bfloat16),
            pltpu.VMEM((2 * rows, width), jnp.float32),
            pltpu.SemaphoreType.DMA((depth // block,)),
        ],
        compiler_params=pltpu.CompilerParams(vmem_limit_bytes=48 * 2**20),
        cost_estimate=pl.CostEstimate(
            flops=4 * rows * depth * width, bytes_accessed=2 * depth * (2 * rows + width), transcendentals=0
        ),
        name="product",
    )(place, ours, theirs, near, far)


def finish_kernel(place_ref, us_ref, back_ref, o_ref):
    def store(gate, up):
        o_ref[...] = (gate / (1.0 + jnp.exp(-gate)) * up).astype(jnp.bfloat16)

    @pl.when(place_ref[1] == 0)
    def _():
        store(us_ref[...], back_ref[...].astype(jnp.float32))

    @pl.when(place_ref[1] != 0)
    def _():
        store(back_ref[...].astype(jnp.float32), us_ref[...])


def finish(place, for_us, back):
    vm = pl.BlockSpec(memory_space=pltpu.VMEM)
    return pl.pallas_call(
        finish_kernel,
        out_shape=jax.ShapeDtypeStruct(back.shape, jnp.bfloat16),
        in_specs=[pl.BlockSpec(memory_space=pltpu.SMEM), vm, vm],
        out_specs=vm,
        compiler_params=pltpu.CompilerParams(vmem_limit_bytes=48 * 2**20),
        name="finish",
    )(place, for_us, back)


def swapped(block, axis):
    return lax.ppermute(block, axis, [(0, 1), (1, 0)])


def from_behind(block, distance):
    devices = range(lax.axis_size(SEQ))
    route = [(i - distance, i) for i in devices if i - distance in devices]
    return lax.ppermute(block, SEQ, route)


def over_heads(tiles):
    return lax.all_to_all(tiles, HEAD, 0, 0, tiled=True)


def norm_kernel(arrived_ref, residual_ref, gain_ref, residual_out_ref, tiles_ref):
    peers, rows, cols = arrived_ref.shape
    gain = gain_ref[...]
    for at in range(0, rows, 8):
        part = pl.ds(at, 8)
        total = arrived_ref[0, part, :].astype(jnp.float32)
        for i in range(1, peers):
            total += arrived_ref[i, part, :].astype(jnp.float32)
        summed = residual_ref[part, :].astype(jnp.float32) + total
        residual_out_ref[part, :] = summed.astype(jnp.bfloat16)
        mean_square = jnp.sum(summed * summed, axis=1, keepdims=True) / cols
        normed = (summed * lax.rsqrt(mean_square + 1e-05) * gain).astype(jnp.bfloat16)
        for i in range(peers):
            tiles_ref[i, part, :] = normed


def normalize(arrived, residual_in, norm_gain):
    vm = pl.BlockSpec(memory_space=pltpu.VMEM)
    return pl.pallas_call(
        norm_kernel,
        out_shape=(
            jax.ShapeDtypeStruct(residual_in.shape, jnp.bfloat16),
            jax.ShapeDtypeStruct(arrived.shape, jnp.bfloat16),
        ),
        in_specs=[vm, vm, vm],
        out_specs=(vm, vm),
        compiler_params=pltpu.CompilerParams(vmem_limit_bytes=24 * 2**20),
        name="normalize",
    )(arrived, residual_in, norm_gain.reshape(1, -1))


def body(queries, key_one, key_two, value_one, value_two, residual_in, out_weight, norm_gain, gate_weight, up_weight):
    rows, _ = queries.shape
    peers = lax.axis_size(HEAD)
    core = lax.axis_index("core").astype(jnp.int32)
    own, far, last, kept, sent = prepare(
        core.reshape(1), key_one, value_one, key_two, value_two, gate_weight, up_weight, 512 - 2 * rows
    )
    mine = jnp.concatenate([kept, swapped(sent, "core")], axis=0)
    near = lax.all_gather(mine, "z", axis=0, tiled=True)
    other = swapped(mine, "xh")
    place = jnp.stack([lax.axis_index("xh").astype(jnp.int32), core])
    rank = lax.axis_index(SEQ).astype(jnp.int32).reshape(1)
    far1 = from_behind(own, 1)
    far2 = from_behind(far, 2)
    far3 = from_behind(last, 3)
    far_weight = lax.all_gather(other, "z", axis=0, tiled=True)
    partial = attend(queries, far3, far2, far1, own, rank, out_weight, 0, 1)
    arrived = over_heads(partial.reshape(peers, rows // peers, -1))
    residual_out, tiles = normalize(arrived, residual_in, norm_gain)
    ours = over_heads(tiles).reshape(rows, -1)
    theirs = swapped(ours, "core")
    for_us, for_them = product(place, ours, theirs, near, far_weight)
    hidden = finish(place, for_us, swapped(for_them, "core"))
    return (residual_out, hidden)


def solution(mesh):
    fine = Mesh(np.asarray(mesh.devices).reshape(8, 2, 2, 4, 2), SEQ + HEAD)
    return jax.shard_map(
        body,
        mesh=fine,
        in_specs=(
            P(SEQ, HEAD),
            P(SEQ, None),
            P(SEQ, None),
            P(SEQ, None),
            P(SEQ, None),
            P(SEQ + HEAD, None),
            P(HEAD, None),
            P(),
            P(SEQ, HEAD),
            P(SEQ, HEAD),
        ),
        out_specs=(P(SEQ + HEAD, None), P(SEQ, HEAD)),
        check_vma=False,
    )
```
